256 devices in a mesh: lon: 64 (over z, x_lo, y), lat: 4 (over x_hi, core).
Axes of the slice: x: 4 (x_hi: 2, x_lo: 2; x = x_hi * 2 + x_lo), y: 4, z: 8, core: 2. Of those that a mesh axis runs over, the one named last changes fastest.
Arguments:
- sketch_bits: int32 [3072, 768, 128], P('lon', 'lat'), may hold values from 0 to 1
- rates: float32 [3072, 8, 768], P('lon', None, 'lat'), may hold values from 0 to 1, as said below
- merid_matrix: bfloat16 [768, 768], P('lat'), as said below
- vert_matrix: bfloat16 [8, 8], replicated, may hold values from -2 to 2
Outputs:
- correlated: bfloat16 [3072, 768, 128], P('lon', 'lat')
The draws below stay inside these ranges and needn't reach their ends.
Inputs may be any that keep to these rules, and one draw needn't show every extreme that they name: `rates`: rates are strictly positive. merid_matrix[j, k] is zero where |j - k| > 96.
All inputs are finite; a program needn't handle non-finite values.
Results may differ from the reference program's by a relative error of at most 0.0057.
Values may be sent and summed in bfloat16 or wider, within the bound.
A program may use at most 128 MiB of HBM per device.

```python
import math
import jax
import jax.numpy as jnp
from jax import lax

LONGITUDE_COUNT = 3072
NLAT = 768
LEV = 8
CH = 128
BAND = 96


def draw_rates(key, part):
    random_subkey_list = jax.random.split(key, 6)
    fast_share = 0.5
    column_shape = (1, LEV, NLAT)
    complete_grid_shape = (LONGITUDE_COUNT, LEV, NLAT)
    is_fast = jax.random.uniform(random_subkey_list[0], column_shape, jnp.float32) < fast_share
    slow_rate = jnp.exp(jax.random.uniform(random_subkey_list[1], column_shape, jnp.float32, math.log(0.1), math.log(0.6))) / LONGITUDE_COUNT
    fast_rate = 1.0 / jax.random.uniform(random_subkey_list[2], column_shape, jnp.float32, 30.0, 50.0)
    baseline_decay_rate = jnp.where(is_fast, fast_rate, slow_rate)
    rate_perturbation = jnp.exp(jax.random.uniform(random_subkey_list[3], complete_grid_shape, jnp.float32, math.log(0.5), math.log(2.0)))
    sudden_spike = jax.random.uniform(random_subkey_list[4], complete_grid_shape, jnp.float32) < 2.0 / LONGITUDE_COUNT
    spike_decay_loss = jax.random.uniform(random_subkey_list[5], complete_grid_shape, jnp.float32, -math.log(0.8), -math.log(0.5))
    final_decay_rates = baseline_decay_rate * rate_perturbation + jnp.where(sudden_spike, spike_decay_loss, 0.0)
    return final_decay_rates.astype(jnp.float32)


def draw_merid_matrix(key, part):
    row_ids = jnp.arange(NLAT, dtype=jnp.int32)[:, None]
    col_ids = jnp.arange(NLAT, dtype=jnp.int32)[None, :]
    distance = jnp.abs(row_ids - col_ids).astype(jnp.float32)
    in_band = (distance <= BAND) & (distance > 0.0)
    noise = jax.random.normal(key, (NLAT, NLAT), jnp.float32)
    off_diag = 0.8 / math.sqrt(BAND) * noise * jnp.exp(-0.25 * distance / BAND)
    result_matrix = jnp.where(distance == 0.0, 1.0, jnp.where(in_band, off_diag, 0.0))
    return result_matrix.astype(jnp.float32).astype(jnp.bfloat16)


def plant(result, key, least, largest):
    dims = result.shape
    place = [jax.random.randint(jax.random.fold_in(key, axis), (), 0, dims[axis]) for axis in range(len(dims))]
    result = result.at[tuple(place)].set(least)
    longest = dims.index(max(dims))
    place[longest] = (place[longest] + 1) % dims[longest]
    return result.at[tuple(place)].set(largest)


def normal_values(rng, extent, deviation, most, kind=jnp.bfloat16):
    array = deviation * jax.random.normal(rng, extent, jnp.float32)
    return jnp.clip(array, min=-most, max=most).astype(kind)


def setup_inputs(seed: int = 0) -> dict:
    seeds = jax.random.split(jax.random.key(seed), 5)
    sketch_bits = plant(jax.random.randint(seeds[0], (LONGITUDE_COUNT, NLAT, CH), 0, 2), jax.random.fold_in(seeds[0], 1), 0, 1).astype(jnp.int32)
    rates = draw_rates(jax.random.fold_in(seeds[4], 71), 0)
    merid_matrix = draw_merid_matrix(jax.random.fold_in(seeds[4], 71), 0)
    vert_matrix = normal_values(seeds[3], (LEV, LEV), LEV ** -0.5, 2.0)
    return {"sketch_bits": sketch_bits, "rates": rates, "merid_matrix": merid_matrix, "vert_matrix": vert_matrix}


def zonal_lines(signs, rate_chan):
    decays = jnp.exp(-rate_chan)
    squared = -jnp.expm1(-2.0 * rate_chan)
    gain_in = jnp.sqrt(squared)
    gain_out = squared / jnp.sqrt(1.0 + decays * decays)
    denominator = -jnp.expm1(-lax.optimization_barrier(jnp.sum(rate_chan, axis=0)))
    zero_state = jnp.zeros(signs.shape[1:], jnp.float32)

    def advance(state_now, inputs):
        factor, source = inputs
        state_now = factor * state_now + source
        return (state_now, state_now)

    def periodic(source, backward):
        end_state, _ = lax.scan(advance, zero_state, (decays, source), reverse=backward)
        _, result_field = lax.scan(advance, end_state / denominator, (decays, source), reverse=backward)
        return result_field
    east_field = periodic(gain_in * signs, False)
    return periodic(gain_out * east_field, True).astype(jnp.bfloat16)

def reference(sketch_bits, rates, merid_matrix, vert_matrix):
    lon_total, lat_total, chan_count = sketch_bits.shape
    levels = vert_matrix.shape[0]
    columns = chan_count // levels
    lat_block = math.gcd(lat_total, 64)

    def zonal_part(block_index):
        first_row = (block_index * lat_block).astype(jnp.int32)
        sign_bits = lax.dynamic_slice_in_dim(sketch_bits, first_row, lat_block, 1)
        part_rates = lax.dynamic_slice_in_dim(rates, first_row, lat_block, 2)
        rate_chan = jnp.repeat(jnp.transpose(part_rates, (0, 2, 1)), columns, axis=2)
        signs = (2 * sign_bits - 1).astype(jnp.float32)
        return zonal_lines(signs, rate_chan)
    zonal_parts = lax.map(zonal_part, jnp.arange(lat_total // lat_block, dtype=jnp.int32))
    zonal_field = jnp.transpose(zonal_parts, (1, 0, 2, 3)).reshape(lon_total, lat_total, chan_count)
    lon_block = math.gcd(lon_total, 32)
    merid_wide = merid_matrix.astype(jnp.float32)
    vert_wide = vert_matrix.astype(jnp.float32)

    def mixing_part(block_index):
        first_row = (block_index * lon_block).astype(jnp.int32)
        lon_rows = lax.dynamic_slice_in_dim(zonal_field, first_row, lon_block, 0).astype(jnp.float32)
        merid_field = jnp.einsum('jk,ikc->ijc', merid_wide, lon_rows).astype(jnp.bfloat16)
        stacked = merid_field.astype(jnp.float32).reshape(lon_block, lat_total, levels, columns)
        result_block = jnp.einsum('pm,ijmc->ijpc', vert_wide, stacked).reshape(lon_block, lat_total, chan_count)
        return result_block.astype(jnp.bfloat16)
    mixed_parts = lax.map(mixing_part, jnp.arange(lon_total // lon_block, dtype=jnp.int32))
    return mixed_parts.reshape(lon_total, lat_total, chan_count)
```

```python
import functools

import jax
import jax.numpy as jnp
from jax import lax
from jax.experimental import pallas as pl
from jax.experimental.pallas import tpu as pltpu
from jax.sharding import PartitionSpec as P

BAND = 96
LANES = 128
F32 = jnp.float32
BF16 = jnp.bfloat16
MESH = pl.DeviceIdType.MESH


def loss_of(rate):
    total = jnp.ones_like(rate)
    for order in range(13, 1, -1):
        total = 1.0 - total * rate * (1.0 / order)
    return rate * total


def spread(tile, index):
    return jnp.take_along_axis(tile, index, axis=1, mode="promise_in_bounds")


def lane_index(rows, first, columns_each):
    lane = lax.broadcasted_iota(jnp.int32, (rows, LANES), 1)
    return lane // columns_each + first


def filter_kernel(
    chunk,
    rates_ref,
    bits_hbm,
    ends_ref,
    inside_ref,
    coef_ref,
    coef_small_ref,
    bits,
    east,
    lev_scratch,
    lat_scratch,
    sems,
):
    lon_here, levels, lat_here = rates_ref.shape
    columns_each = LANES // levels
    per_tile = LANES // levels
    steps = lon_here // chunk
    copies = [
        pltpu.make_async_copy(
            bits_hbm.at[pl.ds(t * chunk, chunk)], bits.at[pl.ds(t * chunk, chunk)], sems.at[t]
        )
        for t in range(steps)
    ]
    for copy in copies:
        copy.start()

    loss = loss_of(rates_ref[...])
    squared = loss * (2.0 - loss)
    decay = 1.0 - loss
    lev_scratch[0] = loss
    lev_scratch[1] = squared / jnp.sqrt(1.0 + decay * decay)
    lat_scratch[0] = loss.reshape(lon_here * levels, lat_here).T
    lat_scratch[1] = jnp.sqrt(squared).reshape(lon_here * levels, lat_here).T
    lat_scratch[2] = lev_scratch[1].reshape(lon_here * levels, lat_here).T

    passed = jnp.ones((levels, lat_here), F32)
    for i in range(lon_here):
        passed = passed - lev_scratch[0, i] * passed
        lev_scratch[2, i] = passed
    coef = jnp.zeros((levels, lat_here), F32)
    lost = jnp.zeros((levels, lat_here), F32)
    for i in reversed(range(lon_here)):
        here = lev_scratch[0, i]
        coef = coef - here * coef + lev_scratch[1, i] * lev_scratch[2, i]
        lost = lost + (here - here * lost)
        lev_scratch[2, i] = coef
        lev_scratch[3, i] = lost
    coef_ref[0] = lev_scratch[2].reshape(lon_here * levels, lat_here).T
    coef_ref[1] = lev_scratch[3].reshape(lon_here * levels, lat_here).T
    coef_small_ref[...] = coef_ref[...].astype(BF16)

    def expanded(which, i):
        column = pl.multiple_of(i // per_tile * LANES, LANES)
        index = lane_index(lat_here, i % per_tile * levels, columns_each)
        return spread(lat_scratch[which, :, pl.ds(column, LANES)], index)

    def forward(i, state):
        gain = expanded(1, i)
        state = state - expanded(0, i) * state + jnp.where(bits[i] > 0, gain, -gain)
        east[i] = state
        return state

    def backward(k, state):
        i = lon_here - 1 - k
        state = state - expanded(0, i) * state + expanded(2, i) * east[i]
        inside_ref[i] = state.astype(BF16)
        return state

    state = jnp.zeros((lat_here, LANES), F32)
    for t in range(steps):
        copies[t].wait()
        state = lax.fori_loop(t * chunk, (t + 1) * chunk, forward, state)
    ends_ref[0] = state
    ends_ref[1] = lax.fori_loop(0, lon_here, backward, jnp.zeros_like(state))
    index = lane_index(lat_here, 0, columns_each)
    lane = lax.broadcasted_iota(jnp.int32, (lat_here, LANES), 1)
    first_half = lane % columns_each < columns_each // 2
    ends_ref[2] = jnp.where(
        first_half,
        spread(coef_ref[1, :, :LANES], index),
        spread(coef_ref[0, :, :LANES], index),
    )


def run_filters(rates, bits):
    lon_here, levels, lat_here = rates.shape
    chunk = 8
    vmem = pl.BlockSpec(memory_space=pltpu.VMEM)
    hbm = pl.BlockSpec(memory_space=pltpu.HBM)
    return pl.pallas_call(
        functools.partial(filter_kernel, chunk),
        name="zonal_filters",
        out_shape=(
            jax.ShapeDtypeStruct((3, lat_here, LANES), F32),
            jax.ShapeDtypeStruct((lon_here, lat_here, LANES), BF16),
            jax.ShapeDtypeStruct((2, lat_here, lon_here * levels), F32),
            jax.ShapeDtypeStruct((2, lat_here, lon_here * levels), BF16),
        ),
        in_specs=[vmem, hbm],
        out_specs=(vmem, vmem, vmem, vmem),
        scratch_shapes=[
            pltpu.VMEM((lon_here, lat_here, LANES), jnp.int32),
            pltpu.VMEM((lon_here, lat_here, LANES), F32),
            pltpu.VMEM((4, lon_here, levels, lat_here), F32),
            pltpu.VMEM((3, lat_here, lon_here * levels), F32),
            pltpu.SemaphoreType.DMA((lon_here // chunk,)),
        ],
        compiler_params=pltpu.CompilerParams(vmem_limit_bytes=40 << 20),
    )(rates, bits)


def unpack(packed, half):
    lane = lax.broadcasted_iota(jnp.int32, packed.shape, 1)
    first_half = lane % (2 * half) < half
    up = pltpu.roll(packed, half, 1)
    down = pltpu.roll(packed, LANES - half, 1)
    return jnp.where(first_half, packed, up), jnp.where(first_half, down, packed)


def compose(near, far):
    loss_a, cross_a, east_a, west_a = near
    loss_b, cross_b, east_b, west_b = far
    keep_a, keep_b = 1.0 - loss_a, 1.0 - loss_b
    return (
        loss_a + keep_a * loss_b,
        cross_a + keep_a * cross_b * keep_a,
        east_b + keep_b * east_a,
        west_a + keep_a * (west_b + cross_b * east_a),
    )


def exchange_kernel(
    inner,
    outer,
    lats,
    half,
    ends_ref,
    inside_hbm,
    coef_hbm,
    entry_ref,
    inside_halo,
    coef_halo,
    parts,
    joined,
    groups,
    solved,
    send_sem,
    recv_sem,
    halo_send,
    halo_recv,
):
    lon = lax.axis_index("lon")
    lat = lax.axis_index("lat")
    place, group = lon % inner, lon // inner
    lat_here = ends_ref.shape[1]
    rows = lat_here // inner
    top_half = inner // 2
    has_prev, has_next = lat > 0, lat < lats - 1
    prev_lat, next_lat = jnp.maximum(lat - 1, 0), jnp.minimum(lat + 1, lats - 1)

    def device(lon_id, lat_id):
        return {"lon": lon_id, "lat": lat_id}

    def mate(k):
        return (place + k) % inner

    def mate_lon(k):
        return group * inner + mate(k)

    def remote_lon(k):
        return (group + k) % outer * inner + place

    barrier = pltpu.get_barrier_semaphore()

    def greet(lon_id, lat_id):
        pl.semaphore_signal(barrier, inc=1, device_id=device(lon_id, lat_id), device_id_type=MESH)

    def greet_mates(k, _):
        greet(mate_lon(k), lat)
        return 0

    def greet_groups(k, _):
        greet(remote_lon(k), lat)
        return 0

    lax.fori_loop(1, inner, greet_mates, 0)
    lax.fori_loop(1, outer, greet_groups, 0)

    @pl.when(has_prev)
    def _():
        def greet_side(k, _):
            greet(group * inner + k, prev_lat)
            return 0

        lax.fori_loop(0, inner, greet_side, 0)

    @pl.when(has_next)
    def _():
        def greet_side(k, _):
            greet(group * inner + k, next_lat)
            return 0

        lax.fori_loop(0, inner, greet_side, 0)

    sides = has_prev.astype(jnp.int32) + has_next.astype(jnp.int32)
    pl.semaphore_wait(barrier, inner - 1 + outer - 1 + inner * sides)

    def part_rows(index):
        return pl.ds(pl.multiple_of(index * rows, rows), rows)

    def part_copy(k):
        return pltpu.make_async_remote_copy(
            src_ref=ends_ref.at[:, part_rows(mate(k)), :],
            dst_ref=parts.at[place],
            send_sem=send_sem.at[0, k],
            recv_sem=recv_sem.at[0, place],
            device_id=device(mate_lon(k), lat),
            device_id_type=MESH,
        )

    def part_arrival(k):
        return pltpu.make_async_remote_copy(
            src_ref=ends_ref.at[:, part_rows(mate(k)), :],
            dst_ref=parts.at[mate(k)],
            send_sem=send_sem.at[0, k],
            recv_sem=recv_sem.at[0, mate(k)],
            device_id=device(mate_lon(k), lat),
            device_id_type=MESH,
        )

    def send_part(k, _):
        part_copy(k).start()
        return 0

    lax.fori_loop(1, inner, send_part, 0)
    parts[place] = ends_ref[:, part_rows(place), :]

    def side_copies(first, slot, lat_id, base):
        return [
            pltpu.make_async_remote_copy(
                src_ref=inside_hbm.at[:, pl.ds(first, BAND), :],
                dst_ref=inside_halo.at[slot],
                send_sem=halo_send.at[base],
                recv_sem=halo_recv.at[slot * 2],
                device_id=device(lon, lat_id),
                device_id_type=MESH,
            ),
            pltpu.make_async_remote_copy(
                src_ref=coef_hbm.at[:, pl.ds(first, BAND), :],
                dst_ref=coef_halo.at[slot],
                send_sem=halo_send.at[base + 1],
                recv_sem=halo_recv.at[slot * 2 + 1],
                device_id=device(lon, lat_id),
                device_id_type=MESH,
            ),
        ]

    @pl.when(has_prev)
    def _():
        for copy in side_copies(0, 1, prev_lat, 0):
            copy.start()

    @pl.when(has_next)
    def _():
        for copy in side_copies(lat_here - BAND, 0, next_lat, 2):
            copy.start()

    def wait_part(k, _):
        part_arrival(k).wait_recv()
        return 0

    lax.fori_loop(1, inner, wait_part, 0)

    def map_of(ref, index):
        value = ref[index]
        loss, cross = unpack(value[2], half)
        return loss, cross, value[0], value[1]

    def join(p, near):
        return compose(near, map_of(parts, p))

    loss, cross, east, west = lax.fori_loop(1, inner, join, map_of(parts, 0))
    lane = lax.broadcasted_iota(jnp.int32, (rows, LANES), 1)
    packed = jnp.where(lane % (2 * half) < half, loss, cross)
    joined[0] = east
    joined[1] = west
    joined[2] = packed

    def group_copy(k):
        return pltpu.make_async_remote_copy(
            src_ref=joined,
            dst_ref=groups.at[group],
            send_sem=send_sem.at[1, k],
            recv_sem=recv_sem.at[1, group],
            device_id=device(remote_lon(k), lat),
            device_id_type=MESH,
        )

    def group_arrival(k):
        other = (group + k) % outer
        return pltpu.make_async_remote_copy(
            src_ref=joined,
            dst_ref=groups.at[other],
            send_sem=send_sem.at[1, k],
            recv_sem=recv_sem.at[1, other],
            device_id=device(remote_lon(k), lat),
            device_id_type=MESH,
        )

    def send_group(k, _):
        group_copy(k).start()
        return 0

    lax.fori_loop(1, outer, send_group, 0)
    groups[group, 0] = east
    groups[group, 1] = west
    groups[group, 2] = packed

    def wait_group(k, _):
        group_arrival(k).wait_recv()
        return 0

    lax.fori_loop(1, outer, wait_group, 0)

    zeros = jnp.zeros((rows, LANES), F32)

    def whole_east(z, carry):
        state, lost = carry
        loss_z, _, east_z, _ = map_of(groups, z)
        return east_z + state - loss_z * state, lost + loss_z - lost * loss_z

    end_state, lost = lax.fori_loop(0, outer, whole_east, (zeros, zeros))
    first_east = end_state / lost

    def whole_west(z, carry):
        state, kept, east_now = carry
        loss_z, cross_z, east_z, west_z = map_of(groups, z)
        keep_z = 1.0 - loss_z
        state = state + kept * (west_z + cross_z * east_now)
        return state, kept * keep_z, east_z + keep_z * east_now

    west_total, _, _ = lax.fori_loop(0, outer, whole_west, (zeros, zeros + 1.0, first_east))
    last_west = west_total / lost

    def to_group(z, state):
        loss_z, _, east_z, _ = map_of(groups, z)
        return east_z + state - loss_z * state

    east_here = lax.fori_loop(0, group, to_group, first_east)

    def west_before(z, carry):
        state, kept, east_now = carry
        loss_z, cross_z, east_z, west_z = map_of(groups, z)
        keep_z = 1.0 - loss_z
        state = state + kept * (west_z + cross_z * east_now)
        return state, kept * keep_z, east_z + keep_z * east_now

    _, _, east_after = lax.fori_loop(group, group + 1, west_before, (zeros, zeros + 1.0, east_here))
    state, kept, _ = lax.fori_loop(group + 1, outer, west_before, (zeros, zeros + 1.0, east_after))
    west_here = state + kept * last_west

    def inner_east(p, state):
        loss_p, _, east_p, _ = map_of(parts, p)
        solved[p, 0] = state
        return east_p + state - loss_p * state

    lax.fori_loop(0, inner, inner_east, east_here)

    def inner_west(k, state):
        p = inner - 1 - k
        loss_p, cross_p, _, west_p = map_of(parts, p)
        solved[p, 1] = state
        return west_p + cross_p * solved[p, 0] + state - loss_p * state

    lax.fori_loop(0, inner, inner_west, west_here)

    own_first = BAND

    def entry_rows(first):
        return pl.ds(pl.multiple_of(first, 8), rows)

    def entry_copy(k):
        return pltpu.make_async_remote_copy(
            src_ref=solved.at[mate(k)],
            dst_ref=entry_ref.at[:, entry_rows(own_first + place * rows), :],
            send_sem=send_sem.at[2, k],
            recv_sem=recv_sem.at[2, place],
            device_id=device(mate_lon(k), lat),
            device_id_type=MESH,
        )

    def entry_arrival(k):
        return pltpu.make_async_remote_copy(
            src_ref=solved.at[mate(k)],
            dst_ref=entry_ref.at[:, entry_rows(own_first + mate(k) * rows), :],
            send_sem=send_sem.at[2, k],
            recv_sem=recv_sem.at[2, mate(k)],
            device_id=device(mate_lon(k), lat),
            device_id_type=MESH,
        )

    def side_copy(p, first, lat_id):
        return pltpu.make_async_remote_copy(
            src_ref=solved.at[p],
            dst_ref=entry_ref.at[:, entry_rows(first), :],
            send_sem=send_sem.at[3, p],
            recv_sem=recv_sem.at[3, place],
            device_id=device(group * inner + p, lat_id),
            device_id_type=MESH,
        )

    def side_arrival(p, first):
        return pltpu.make_async_remote_copy(
            src_ref=solved.at[p],
            dst_ref=entry_ref.at[:, entry_rows(first), :],
            send_sem=send_sem.at[3, p],
            recv_sem=recv_sem.at[3, p],
            device_id=device(group * inner + p, lat),
            device_id_type=MESH,
        )

    below = own_first + lat_here

    def send_entry(k, _):
        entry_copy(k).start()
        return 0

    to_prev = jnp.logical_and(place < top_half, has_prev)
    to_next = jnp.logical_and(place >= top_half, has_next)
    prev_first = below + jnp.minimum(place, top_half - 1) * rows
    next_first = jnp.maximum(place - top_half, 0) * rows

    lax.fori_loop(1, inner, send_entry, 0)

    @pl.when(to_prev)
    def _():
        def send_side(p, _):
            side_copy(p, prev_first, prev_lat).start()
            return 0

        lax.fori_loop(0, inner, send_side, 0)

    @pl.when(to_next)
    def _():
        def send_side(p, _):
            side_copy(p, next_first, next_lat).start()
            return 0

        lax.fori_loop(0, inner, send_side, 0)

    entry_ref[:, entry_rows(own_first + place * rows), :] = solved[place]

    def wait_entry(k, _):
        entry_arrival(k).wait_recv()
        return 0

    lax.fori_loop(1, inner, wait_entry, 0)

    @pl.when(has_next)
    def _():
        def wait_side(p, _):
            side_arrival(p, below + p * rows).wait_recv()
            return 0

        lax.fori_loop(0, top_half, wait_side, 0)

    @pl.when(has_prev)
    def _():
        def wait_side(p, _):
            side_arrival(p, (p - top_half) * rows).wait_recv()
            return 0

        lax.fori_loop(top_half, inner, wait_side, 0)

    @pl.when(has_prev)
    def _():
        for copy in side_copies(0, 0, prev_lat, 0):
            copy.wait_recv()
        for copy in side_copies(0, 1, prev_lat, 0):
            copy.wait_send()

    @pl.when(has_next)
    def _():
        for copy in side_copies(lat_here - BAND, 1, next_lat, 2):
            copy.wait_recv()
        for copy in side_copies(lat_here - BAND, 0, next_lat, 2):
            copy.wait_send()

    def drain_inner(k, _):
        part_copy(k).wait_send()
        entry_copy(k).wait_send()
        return 0

    def drain_outer(k, _):
        group_copy(k).wait_send()
        return 0

    lax.fori_loop(1, inner, drain_inner, 0)
    lax.fori_loop(1, outer, drain_outer, 0)

    @pl.when(to_prev)
    def _():
        def drain(p, _):
            side_copy(p, prev_first, prev_lat).wait_send()
            return 0

        lax.fori_loop(0, inner, drain, 0)

    @pl.when(to_next)
    def _():
        def drain(p, _):
            side_copy(p, next_first, next_lat).wait_send()
            return 0

        lax.fori_loop(0, inner, drain, 0)


def run_exchange(mesh, levels, ends, inside, coef_small):
    lons, lats = mesh.shape["lon"], mesh.shape["lat"]
    inner = 8 if lons > 16 else 2
    outer = lons // inner
    _, lat_here, _ = ends.shape
    lon_here = inside.shape[0]
    rows = lat_here // inner
    half = LANES // levels // 2
    vmem = pl.BlockSpec(memory_space=pltpu.VMEM)
    hbm = pl.BlockSpec(memory_space=pl.ANY)
    most = max(inner, outer)
    return pl.pallas_call(
        functools.partial(exchange_kernel, inner, outer, lats, half),
        name="loop_exchange",
        out_shape=(
            jax.ShapeDtypeStruct((2, lat_here + 2 * BAND, LANES), F32),
            jax.ShapeDtypeStruct((2, lon_here, BAND, LANES), BF16),
            jax.ShapeDtypeStruct((2, 2, BAND, coef_small.shape[2]), BF16),
        ),
        in_specs=[vmem, hbm, hbm],
        out_specs=(vmem, hbm, hbm),
        scratch_shapes=[
            pltpu.VMEM((inner, 3, rows, LANES), F32),
            pltpu.VMEM((3, rows, LANES), F32),
            pltpu.VMEM((outer, 3, rows, LANES), F32),
            pltpu.VMEM((inner, 2, rows, LANES), F32),
            pltpu.SemaphoreType.DMA((4, most)),
            pltpu.SemaphoreType.DMA((4, most)),
            pltpu.SemaphoreType.DMA((4,)),
            pltpu.SemaphoreType.DMA((4,)),
        ],
        compiler_params=pltpu.CompilerParams(
            collective_id=0, has_side_effects=True, vmem_limit_bytes=16 << 20
        ),
    )(ends, inside, coef_small)


def combine_kernel(
    batch,
    levels,
    sides_ref,
    inside_ref,
    top_ref,
    bottom_ref,
    coef_ref,
    coef_top_ref,
    coef_bottom_ref,
    entry_ref,
    band_ref,
    level_ref,
    out_ref,
    zonal,
):
    columns_each = LANES // levels
    per_tile = LANES // levels
    lat_here = inside_ref.shape[1]
    below = BAND + lat_here
    first = pl.program_id(0) * batch % per_tile
    has_top, has_bottom = sides_ref[0] > 0, sides_ref[1] > 0

    def field(inside, coef, count, low, j):
        index = lane_index(count, (first + j) * levels, columns_each)
        east = entry_ref[0, pl.ds(low, count), :]
        west = entry_ref[1, pl.ds(low, count), :]
        cross = spread(coef[0].astype(F32), index)
        lost = spread(coef[1].astype(F32), index)
        return inside.astype(F32) + cross * east + (west - lost * west)

    zeros = jnp.zeros((BAND, LANES), F32)
    for pair in range(batch // 2):
        for side in range(2):
            j = 2 * pair + side
            lanes = pl.ds(side * LANES, LANES)
            upper = field(top_ref[0, j], coef_top_ref[0], BAND, 0, j)
            lower = field(bottom_ref[0, j], coef_bottom_ref[0], BAND, below, j)
            zonal[pair % 2, pl.ds(0, BAND), lanes] = jnp.where(has_top, upper, zeros).astype(BF16)
            zonal[pair % 2, pl.ds(BAND, lat_here), lanes] = field(
                inside_ref[j], coef_ref, lat_here, BAND, j
            ).astype(BF16)
            zonal[pair % 2, pl.ds(below, BAND), lanes] = jnp.where(
                has_bottom, lower, zeros
            ).astype(BF16)
        merid = jnp.dot(
            band_ref[...], zonal[pair % 2], preferred_element_type=F32
        ).astype(BF16)
        for side in range(2):
            out_ref[2 * pair + side] = jnp.dot(
                merid[:, side * LANES : (side + 1) * LANES],
                level_ref[...],
                preferred_element_type=F32,
            ).astype(BF16)


def run_combine(sides, inside, inside_halo, coef, coef_halo, entry, band_tile, level_map, levels):
    lon_here, lat_here, _ = inside.shape
    batch = 8
    per_tile = LANES // levels

    def tile_of(t):
        return t * batch // per_tile

    return pl.pallas_call(
        functools.partial(combine_kernel, batch, levels),
        name="band_product",
        grid=(lon_here // batch,),
        out_shape=jax.ShapeDtypeStruct((lon_here, lat_here, LANES), BF16),
        in_specs=[
            pl.BlockSpec(memory_space=pltpu.SMEM),
            pl.BlockSpec((batch, lat_here, LANES), lambda t: (t, 0, 0)),
            pl.BlockSpec((1, batch, BAND, LANES), lambda t: (0, t, 0, 0)),
            pl.BlockSpec((1, batch, BAND, LANES), lambda t: (1, t, 0, 0)),
            pl.BlockSpec((2, lat_here, LANES), lambda t: (0, 0, tile_of(t))),
            pl.BlockSpec((1, 2, BAND, LANES), lambda t: (0, 0, 0, tile_of(t))),
            pl.BlockSpec((1, 2, BAND, LANES), lambda t: (1, 0, 0, tile_of(t))),
            pl.BlockSpec((2, lat_here + 2 * BAND, LANES), lambda t: (0, 0, 0)),
            pl.BlockSpec(band_tile.shape, lambda t: (0, 0)),
            pl.BlockSpec(level_map.shape, lambda t: (0, 0)),
        ],
        out_specs=pl.BlockSpec((batch, lat_here, LANES), lambda t: (t, 0, 0)),
        scratch_shapes=[pltpu.VMEM((2, lat_here + 2 * BAND, 2 * LANES), BF16)],
        compiler_params=pltpu.CompilerParams(vmem_limit_bytes=24 << 20),
    )(
        sides,
        inside,
        inside_halo,
        inside_halo,
        coef,
        coef_halo,
        coef_halo,
        entry,
        band_tile,
        level_map,
    )


def solution(mesh):
    def per_device(sketch_bits, rates, merid_matrix, vert_matrix):
        lats = mesh.shape["lat"]
        levels = vert_matrix.shape[0]
        lat_here = sketch_bits.shape[1]
        lat = lax.axis_index("lat")
        padded_rows = jnp.pad(merid_matrix, ((0, 0), (BAND, BAND)))
        band_tile = lax.dynamic_slice_in_dim(
            padded_rows, lat * lat_here, lat_here + 2 * BAND, 1
        )
        ident_cols = jnp.eye(LANES // levels, dtype=BF16)
        level_map = (vert_matrix.T[:, None, :, None] * ident_cols[None, :, None, :]).reshape(
            LANES, LANES
        )
        sides = jnp.stack([lat > 0, lat < lats - 1]).astype(jnp.int32)
        ends, inside, coef, coef_small = run_filters(rates, sketch_bits)
        entry, inside_halo, coef_halo = run_exchange(mesh, levels, ends, inside, coef_small)
        return run_combine(
            sides, inside, inside_halo, coef, coef_halo, entry, band_tile, level_map, levels
        )

    in_specs = (P("lon", "lat", None), P("lon", None, "lat"), P("lat", None), P())
    out_specs = P("lon", "lat", None)
    return jax.shard_map(
        per_device, mesh=mesh, in_specs=in_specs, out_specs=out_specs, check_vma=False
    )
```

```python
import functools

import jax
import jax.numpy as jnp
from jax import lax
from jax.experimental import pallas as pl
from jax.experimental.pallas import tpu as pltpu
from jax.sharding import PartitionSpec as P

BAND = 96
LANES = 128
F32 = jnp.float32
BF16 = jnp.bfloat16
MESH = pl.DeviceIdType.MESH


def loss_of(rate):
    factors = [1.0]
    for order in range(2, 13):
        factors.append(-factors[-1] / order)
    total = jnp.full_like(rate, factors[-1])
    for factor in reversed(factors[:-1]):
        total = total * rate + factor
    return rate * total


def spread(tile, index):
    return jnp.take_along_axis(tile, index, axis=1, mode="promise_in_bounds")


def lane_index(rows, first, columns_each):
    lane = lax.broadcasted_iota(jnp.int32, (rows, LANES), 1)
    return lane // columns_each + first


def filter_kernel(
    block,
    rates_hbm,
    bits_hbm,
    ends_ref,
    inside_ref,
    coef_ref,
    coef_small_ref,
    rates_ref,
    bits,
    east,
    decay_chan,
    lev_scratch,
    lat_scratch,
    total,
    sems,
):
    lon_here, levels, lat_here = rates_ref.shape
    columns_each = LANES // levels
    per_tile = LANES // levels
    tiles = lon_here // per_tile
    blocks = lat_here // block
    rates_copy = pltpu.make_async_copy(rates_hbm, rates_ref, sems.at[tiles])
    rates_copy.start()
    copies = [
        pltpu.make_async_copy(
            bits_hbm.at[pl.ds(t * per_tile, per_tile)],
            bits.at[pl.ds(t * per_tile, per_tile)],
            sems.at[t],
        )
        for t in range(tiles)
    ]
    for copy in copies:
        copy.start()
    rates_copy.wait()

    loss = loss_of(rates_ref[...])
    squared = loss * (2.0 - loss)
    decay = 1.0 - loss
    gain_out = squared * lax.rsqrt(1.0 + decay * decay)
    lev_scratch[0] = decay
    lev_scratch[1] = gain_out
    lev_scratch[4] = loss
    lat_scratch[0] = decay.reshape(lon_here * levels, lat_here).T
    lat_scratch[1] = jnp.sqrt(squared).reshape(lon_here * levels, lat_here).T
    lat_scratch[2] = gain_out.reshape(lon_here * levels, lat_here).T

    passed = jnp.ones((levels, lat_here), F32)
    lost = jnp.zeros((levels, lat_here), F32)
    for i in range(lon_here):
        passed = lev_scratch[0, i] * passed
        lost = lost + lev_scratch[4, i] * (1.0 - lost)
        lev_scratch[2, i] = passed
    coef = jnp.zeros((levels, lat_here), F32)
    kept = jnp.ones((levels, lat_here), F32)
    for i in reversed(range(lon_here)):
        here = lev_scratch[0, i]
        coef = here * coef + lev_scratch[1, i] * lev_scratch[2, i]
        kept = here * kept
        lev_scratch[2, i] = coef
        lev_scratch[3, i] = kept
    coef_ref[0] = lev_scratch[2].reshape(lon_here * levels, lat_here).T
    coef_ref[1] = lev_scratch[3].reshape(lon_here * levels, lat_here).T
    coef_small_ref[...] = coef_ref[...].astype(BF16)
    total[:, :levels] = lost.T

    def rows_of(b):
        return pl.ds(pl.multiple_of(b * block, block), block)

    ends_ref[0] = jnp.zeros((lat_here, LANES), F32)
    ends_ref[1] = jnp.zeros((lat_here, LANES), F32)
    for t in range(tiles):
        copies[t].wait()
        lanes = pl.ds(t * LANES, LANES)

        def forward(b, _):
            rows = rows_of(b)
            decays, gains = lat_scratch[0, rows, lanes], lat_scratch[1, rows, lanes]
            state = ends_ref[0, rows, :]
            for j in range(per_tile):
                i = t * per_tile + j
                index = lane_index(block, j * levels, columns_each)
                gain = spread(gains, index)
                decay = spread(decays, index)
                decay_chan[i, rows, :] = decay
                state = decay * state + jnp.where(bits[i, rows, :] > 0, gain, -gain)
                east[i, rows, :] = state
            ends_ref[0, rows, :] = state
            return 0

        lax.fori_loop(0, blocks, forward, 0)

    for t in reversed(range(tiles)):
        lanes = pl.ds(t * LANES, LANES)

        def backward(b, _):
            rows = rows_of(b)
            gains = lat_scratch[2, rows, lanes]
            state = ends_ref[1, rows, :]
            for j in reversed(range(per_tile)):
                i = t * per_tile + j
                index = lane_index(block, j * levels, columns_each)
                state = decay_chan[i, rows, :] * state + spread(gains, index) * east[i, rows, :]
                inside_ref[i, rows, :] = state.astype(BF16)
            ends_ref[1, rows, :] = state
            return 0

        lax.fori_loop(0, blocks, backward, 0)

    index = lane_index(lat_here, 0, columns_each)
    lane = lax.broadcasted_iota(jnp.int32, (lat_here, LANES), 1)
    first_half = lane % columns_each < columns_each // 2
    ends_ref[2] = jnp.where(
        first_half, spread(total[...], index), spread(coef_ref[0, :, :LANES], index)
    )


def run_filters(rates, bits):
    lon_here, levels, lat_here = rates.shape
    vmem = pl.BlockSpec(memory_space=pltpu.VMEM)
    hbm = pl.BlockSpec(memory_space=pltpu.HBM)
    columns = lon_here * levels
    return pl.pallas_call(
        functools.partial(filter_kernel, 64),
        name="zonal_filters",
        out_shape=(
            jax.ShapeDtypeStruct((3, lat_here, LANES), F32),
            jax.ShapeDtypeStruct((lon_here, lat_here, LANES), BF16),
            jax.ShapeDtypeStruct((2, lat_here, columns), F32),
            jax.ShapeDtypeStruct((2, lat_here, columns), BF16),
        ),
        in_specs=[hbm, hbm],
        out_specs=(vmem, vmem, vmem, vmem),
        scratch_shapes=[
            pltpu.VMEM((lon_here, levels, lat_here), F32),
            pltpu.VMEM((lon_here, lat_here, LANES), jnp.int32),
            pltpu.VMEM((lon_here, lat_here, LANES), F32),
            pltpu.VMEM((lon_here, lat_here, LANES), F32),
            pltpu.VMEM((5, lon_here, levels, lat_here), F32),
            pltpu.VMEM((3, lat_here, columns), F32),
            pltpu.VMEM((lat_here, LANES), F32),
            pltpu.SemaphoreType.DMA((columns // LANES + 1,)),
        ],
        compiler_params=pltpu.CompilerParams(vmem_limit_bytes=40 << 20),
    )(
        pltpu.with_memory_space_constraint(rates, pltpu.HBM),
        pltpu.with_memory_space_constraint(bits, pltpu.HBM),
    )


def unpack(packed, half):
    lane = lax.broadcasted_iota(jnp.int32, packed.shape, 1)
    first_half = lane % (2 * half) < half
    up = pltpu.roll(packed, half, 1)
    down = pltpu.roll(packed, LANES - half, 1)
    return jnp.where(first_half, packed, up), jnp.where(first_half, down, packed)


def compose(near, far):
    loss_a, cross_a, east_a, west_a = near
    loss_b, cross_b, east_b, west_b = far
    keep_a, keep_b = 1.0 - loss_a, 1.0 - loss_b
    return (
        loss_a + keep_a * loss_b,
        cross_a + keep_a * cross_b * keep_a,
        east_b + keep_b * east_a,
        west_a + keep_a * (west_b + cross_b * east_a),
    )


def exchange_kernel(
    inner,
    outer,
    lats,
    half,
    ends_ref,
    inside_hbm,
    coef_hbm,
    merid_ref,
    vert_ref,
    entry_ref,
    inside_halo,
    coef_halo,
    band_ref,
    level_ref,
    coef_landing,
    parts,
    joined,
    groups,
    solved,
    send_sem,
    recv_sem,
    halo_send,
    halo_recv,
):
    lon = lax.axis_index("lon")
    lat = lax.axis_index("lat")
    place, group = lon % inner, lon // inner
    lat_here = ends_ref.shape[1]
    rows = lat_here // inner
    top_half = inner // 2
    has_prev, has_next = lat > 0, lat < lats - 1
    prev_lat, next_lat = jnp.maximum(lat - 1, 0), jnp.minimum(lat + 1, lats - 1)

    def device(lon_id, lat_id):
        return {"lon": lon_id, "lat": lat_id}

    def mate(k):
        return (place + k) % inner

    def mate_lon(k):
        return group * inner + mate(k)

    def remote_lon(k):
        return (group + k) % outer * inner + place

    barrier = pltpu.get_barrier_semaphore()

    def greet(lon_id, lat_id):
        pl.semaphore_signal(barrier, inc=1, device_id=device(lon_id, lat_id), device_id_type=MESH)

    def greet_mates(k, _):
        greet(mate_lon(k), lat)
        return 0

    def greet_groups(k, _):
        greet(remote_lon(k), lat)
        return 0

    lax.fori_loop(1, inner, greet_mates, 0)
    lax.fori_loop(1, outer, greet_groups, 0)

    @pl.when(has_prev)
    def _():
        def greet_side(k, _):
            greet(group * inner + k, prev_lat)
            return 0

        lax.fori_loop(0, inner, greet_side, 0)

    @pl.when(has_next)
    def _():
        def greet_side(k, _):
            greet(group * inner + k, next_lat)
            return 0

        lax.fori_loop(0, inner, greet_side, 0)

    lat_all = merid_ref.shape[1]
    spans = (lat_all, lat_here + 2 * BAND)
    source = lax.broadcasted_iota(jnp.int32, spans, 0)
    target = lax.broadcasted_iota(jnp.int32, spans, 1)
    pick = jnp.where(source - target == lat * lat_here - BAND, 1.0, 0.0).astype(BF16)
    band_ref[...] = jnp.dot(merid_ref[...], pick, preferred_element_type=F32).astype(BF16)
    levels = vert_ref.shape[0]
    columns_each = LANES // levels
    column = lax.broadcasted_iota(jnp.int32, (LANES, levels), 0)
    level = lax.broadcasted_iota(jnp.int32, (LANES, levels), 1)
    member = jnp.where(column // columns_each == level, 1.0, 0.0).astype(BF16)
    along = (((1,), (1,)), ((), ()))
    by_row = lax.dot_general(member, vert_ref[...], along, preferred_element_type=F32)
    full = lax.dot_general(by_row.astype(BF16), member, along, preferred_element_type=F32)
    row = lax.broadcasted_iota(jnp.int32, (LANES, LANES), 0)
    col = lax.broadcasted_iota(jnp.int32, (LANES, LANES), 1)
    same = row % columns_each == col % columns_each
    level_ref[...] = jnp.where(same, full, 0.0).astype(BF16)

    def clear(slot, first):
        def clear_lon(i, _):
            inside_halo[slot, i] = jnp.zeros(inside_halo.shape[2:], BF16)
            return 0

        lax.fori_loop(0, inside_halo.shape[1], clear_lon, 0)
        coef_halo[slot] = jnp.zeros(coef_halo.shape[1:], F32)
        entry_ref[:, pl.ds(first, BAND), :] = jnp.zeros((2, BAND, LANES), F32)

    @pl.when(jnp.logical_not(has_prev))
    def _():
        clear(0, 0)

    @pl.when(jnp.logical_not(has_next))
    def _():
        clear(1, BAND + lat_here)

    sides = has_prev.astype(jnp.int32) + has_next.astype(jnp.int32)
    pl.semaphore_wait(barrier, inner - 1 + outer - 1 + inner * sides)

    def part_rows(index):
        return pl.ds(pl.multiple_of(index * rows, rows), rows)

    def part_copy(k):
        return pltpu.make_async_remote_copy(
            src_ref=ends_ref.at[:, part_rows(mate(k)), :],
            dst_ref=parts.at[place],
            send_sem=send_sem.at[0, k],
            recv_sem=recv_sem.at[0, place],
            device_id=device(mate_lon(k), lat),
            device_id_type=MESH,
        )

    def part_arrival(k):
        return pltpu.make_async_remote_copy(
            src_ref=ends_ref.at[:, part_rows(mate(k)), :],
            dst_ref=parts.at[mate(k)],
            send_sem=send_sem.at[0, k],
            recv_sem=recv_sem.at[0, mate(k)],
            device_id=device(mate_lon(k), lat),
            device_id_type=MESH,
        )

    def send_part(k, _):
        part_copy(k).start()
        return 0

    lax.fori_loop(1, inner, send_part, 0)
    parts[place] = ends_ref[:, part_rows(place), :]

    def side_copies(first, slot, lat_id, base):
        return [
            pltpu.make_async_remote_copy(
                src_ref=inside_hbm.at[:, pl.ds(first, BAND), :],
                dst_ref=inside_halo.at[slot],
                send_sem=halo_send.at[base],
                recv_sem=halo_recv.at[slot * 2],
                device_id=device(lon, lat_id),
                device_id_type=MESH,
            ),
            pltpu.make_async_remote_copy(
                src_ref=coef_hbm.at[:, pl.ds(first, BAND), :],
                dst_ref=coef_landing.at[slot],
                send_sem=halo_send.at[base + 1],
                recv_sem=halo_recv.at[slot * 2 + 1],
                device_id=device(lon, lat_id),
                device_id_type=MESH,
            ),
        ]

    @pl.when(has_prev)
    def _():
        for copy in side_copies(0, 1, prev_lat, 0):
            copy.start()

    @pl.when(has_next)
    def _():
        for copy in side_copies(lat_here - BAND, 0, next_lat, 2):
            copy.start()

    def wait_part(k, _):
        part_arrival(k).wait_recv()
        return 0

    lax.fori_loop(1, inner, wait_part, 0)

    def map_of(ref, index):
        value = ref[index]
        loss, cross = unpack(value[2], half)
        return loss, cross, value[0], value[1]

    def join(p, near):
        return compose(near, map_of(parts, p))

    loss, cross, east, west = lax.fori_loop(1, inner, join, map_of(parts, 0))
    lane = lax.broadcasted_iota(jnp.int32, (rows, LANES), 1)
    packed = jnp.where(lane % (2 * half) < half, loss, cross)
    joined[0] = east
    joined[1] = west
    joined[2] = packed

    def group_copy(k):
        return pltpu.make_async_remote_copy(
            src_ref=joined,
            dst_ref=groups.at[group],
            send_sem=send_sem.at[1, k],
            recv_sem=recv_sem.at[1, group],
            device_id=device(remote_lon(k), lat),
            device_id_type=MESH,
        )

    def group_arrival(k):
        other = (group + k) % outer
        return pltpu.make_async_remote_copy(
            src_ref=joined,
            dst_ref=groups.at[other],
            send_sem=send_sem.at[1, k],
            recv_sem=recv_sem.at[1, other],
            device_id=device(remote_lon(k), lat),
            device_id_type=MESH,
        )

    def send_group(k, _):
        group_copy(k).start()
        return 0

    lax.fori_loop(1, outer, send_group, 0)
    groups[group, 0] = east
    groups[group, 1] = west
    groups[group, 2] = packed

    def wait_group(k, _):
        group_arrival(k).wait_recv()
        return 0

    lax.fori_loop(1, outer, wait_group, 0)

    zeros = jnp.zeros((rows, LANES), F32)

    def whole_east(z, carry):
        state, lost = carry
        loss_z, _, east_z, _ = map_of(groups, z)
        return east_z + state - loss_z * state, lost + loss_z - lost * loss_z

    end_state, lost = lax.fori_loop(0, outer, whole_east, (zeros, zeros))
    first_east = end_state / lost

    def whole_west(z, carry):
        state, kept, east_now = carry
        loss_z, cross_z, east_z, west_z = map_of(groups, z)
        keep_z = 1.0 - loss_z
        state = state + kept * (west_z + cross_z * east_now)
        return state, kept * keep_z, east_z + keep_z * east_now

    west_total, _, _ = lax.fori_loop(0, outer, whole_west, (zeros, zeros + 1.0, first_east))
    last_west = west_total / lost

    def to_group(z, state):
        loss_z, _, east_z, _ = map_of(groups, z)
        return east_z + state - loss_z * state

    east_here = lax.fori_loop(0, group, to_group, first_east)

    def west_before(z, carry):
        state, kept, east_now = carry
        loss_z, cross_z, east_z, west_z = map_of(groups, z)
        keep_z = 1.0 - loss_z
        state = state + kept * (west_z + cross_z * east_now)
        return state, kept * keep_z, east_z + keep_z * east_now

    _, _, east_after = lax.fori_loop(group, group + 1, west_before, (zeros, zeros + 1.0, east_here))
    state, kept, _ = lax.fori_loop(group + 1, outer, west_before, (zeros, zeros + 1.0, east_after))
    west_here = state + kept * last_west

    def inner_east(p, state):
        loss_p, _, east_p, _ = map_of(parts, p)
        solved[p, 0] = state
        return east_p + state - loss_p * state

    lax.fori_loop(0, inner, inner_east, east_here)

    def inner_west(k, state):
        p = inner - 1 - k
        loss_p, cross_p, _, west_p = map_of(parts, p)
        solved[p, 1] = state
        return west_p + cross_p * solved[p, 0] + state - loss_p * state

    lax.fori_loop(0, inner, inner_west, west_here)

    own_first = BAND

    def entry_rows(first):
        return pl.ds(pl.multiple_of(first, 8), rows)

    def entry_copy(k):
        return pltpu.make_async_remote_copy(
            src_ref=solved.at[mate(k)],
            dst_ref=entry_ref.at[:, entry_rows(own_first + place * rows), :],
            send_sem=send_sem.at[2, k],
            recv_sem=recv_sem.at[2, place],
            device_id=device(mate_lon(k), lat),
            device_id_type=MESH,
        )

    def entry_arrival(k):
        return pltpu.make_async_remote_copy(
            src_ref=solved.at[mate(k)],
            dst_ref=entry_ref.at[:, entry_rows(own_first + mate(k) * rows), :],
            send_sem=send_sem.at[2, k],
            recv_sem=recv_sem.at[2, mate(k)],
            device_id=device(mate_lon(k), lat),
            device_id_type=MESH,
        )

    def side_copy(p, first, lat_id):
        return pltpu.make_async_remote_copy(
            src_ref=solved.at[p],
            dst_ref=entry_ref.at[:, entry_rows(first), :],
            send_sem=send_sem.at[3, p],
            recv_sem=recv_sem.at[3, place],
            device_id=device(group * inner + p, lat_id),
            device_id_type=MESH,
        )

    def side_arrival(p, first):
        return pltpu.make_async_remote_copy(
            src_ref=solved.at[p],
            dst_ref=entry_ref.at[:, entry_rows(first), :],
            send_sem=send_sem.at[3, p],
            recv_sem=recv_sem.at[3, p],
            device_id=device(group * inner + p, lat),
            device_id_type=MESH,
        )

    below = own_first + lat_here

    def send_entry(k, _):
        entry_copy(k).start()
        return 0

    to_prev = jnp.logical_and(place < top_half, has_prev)
    to_next = jnp.logical_and(place >= top_half, has_next)
    prev_first = below + jnp.minimum(place, top_half - 1) * rows
    next_first = jnp.maximum(place - top_half, 0) * rows

    lax.fori_loop(1, inner, send_entry, 0)

    @pl.when(to_prev)
    def _():
        def send_side(p, _):
            side_copy(p, prev_first, prev_lat).start()
            return 0

        lax.fori_loop(0, inner, send_side, 0)

    @pl.when(to_next)
    def _():
        def send_side(p, _):
            side_copy(p, next_first, next_lat).start()
            return 0

        lax.fori_loop(0, inner, send_side, 0)

    entry_ref[:, entry_rows(own_first + place * rows), :] = solved[place]

    def wait_entry(k, _):
        entry_arrival(k).wait_recv()
        return 0

    lax.fori_loop(1, inner, wait_entry, 0)

    @pl.when(has_next)
    def _():
        def wait_side(p, _):
            side_arrival(p, below + p * rows).wait_recv()
            return 0

        lax.fori_loop(0, top_half, wait_side, 0)

    @pl.when(has_prev)
    def _():
        def wait_side(p, _):
            side_arrival(p, (p - top_half) * rows).wait_recv()
            return 0

        lax.fori_loop(top_half, inner, wait_side, 0)

    @pl.when(has_prev)
    def _():
        inside_copy, coef_copy = side_copies(0, 0, prev_lat, 0)
        coef_copy.wait_recv()
        coef_halo[0] = coef_landing[0].astype(F32)
        inside_copy.wait_recv()
        for copy in side_copies(0, 1, prev_lat, 0):
            copy.wait_send()

    @pl.when(has_next)
    def _():
        inside_copy, coef_copy = side_copies(lat_here - BAND, 1, next_lat, 2)
        coef_copy.wait_recv()
        coef_halo[1] = coef_landing[1].astype(F32)
        inside_copy.wait_recv()
        for copy in side_copies(lat_here - BAND, 0, next_lat, 2):
            copy.wait_send()

    def drain_inner(k, _):
        part_copy(k).wait_send()
        entry_copy(k).wait_send()
        return 0

    def drain_outer(k, _):
        group_copy(k).wait_send()
        return 0

    lax.fori_loop(1, inner, drain_inner, 0)
    lax.fori_loop(1, outer, drain_outer, 0)

    @pl.when(to_prev)
    def _():
        def drain(p, _):
            side_copy(p, prev_first, prev_lat).wait_send()
            return 0

        lax.fori_loop(0, inner, drain, 0)

    @pl.when(to_next)
    def _():
        def drain(p, _):
            side_copy(p, next_first, next_lat).wait_send()
            return 0

        lax.fori_loop(0, inner, drain, 0)


def run_exchange(mesh, levels, ends, inside, coef_small, merid, vert):
    lons, lats = mesh.shape["lon"], mesh.shape["lat"]
    inner = 8 if lons > 16 else 2
    outer = lons // inner
    _, lat_here, _ = ends.shape
    lon_here = inside.shape[0]
    rows = lat_here // inner
    half = LANES // levels // 2
    vmem = pl.BlockSpec(memory_space=pltpu.VMEM)
    hbm = pl.BlockSpec(memory_space=pl.ANY)
    most = max(inner, outer)
    return pl.pallas_call(
        functools.partial(exchange_kernel, inner, outer, lats, half),
        name="loop_exchange",
        out_shape=(
            jax.ShapeDtypeStruct((2, lat_here + 2 * BAND, LANES), F32),
            jax.ShapeDtypeStruct((2, lon_here, BAND, LANES), BF16),
            jax.ShapeDtypeStruct((2, 2, BAND, coef_small.shape[2]), F32),
            jax.ShapeDtypeStruct((lat_here, lat_here + 2 * BAND), BF16),
            jax.ShapeDtypeStruct((LANES, LANES), BF16),
        ),
        in_specs=[vmem, hbm, hbm, vmem, vmem],
        out_specs=(vmem, vmem, vmem, vmem, vmem),
        scratch_shapes=[
            pltpu.VMEM((2, 2, BAND, coef_small.shape[2]), BF16),
            pltpu.VMEM((inner, 3, rows, LANES), F32),
            pltpu.VMEM((3, rows, LANES), F32),
            pltpu.VMEM((outer, 3, rows, LANES), F32),
            pltpu.VMEM((inner, 2, rows, LANES), F32),
            pltpu.SemaphoreType.DMA((4, most)),
            pltpu.SemaphoreType.DMA((4, most)),
            pltpu.SemaphoreType.DMA((4,)),
            pltpu.SemaphoreType.DMA((4,)),
        ],
        compiler_params=pltpu.CompilerParams(
            collective_id=0, has_side_effects=True, vmem_limit_bytes=16 << 20
        ),
    )(ends, inside, coef_small, merid, vert)


def combine_kernel(
    batch,
    levels,
    inside_ref,
    top_ref,
    bottom_ref,
    coef_ref,
    coef_top_ref,
    coef_bottom_ref,
    entry_ref,
    band_ref,
    level_ref,
    out_ref,
    zonal,
):
    columns_each = LANES // levels
    per_tile = LANES // levels
    lat_here = inside_ref.shape[1]
    below = BAND + lat_here
    first = pl.program_id(0) * batch % per_tile

    def field(inside, coef, count, low, j):
        index = lane_index(count, (first + j) * levels, columns_each)
        rows = pl.ds(low, count)
        east = spread(coef[0], index) * entry_ref[0, rows, :]
        west = spread(coef[1], index) * entry_ref[1, rows, :]
        return (inside.astype(F32) + east + west).astype(BF16)

    for pair in range(batch // 2):
        held = zonal.at[pair % 2]
        for side in range(2):
            j = 2 * pair + side
            lanes = pl.ds(side * LANES, LANES)
            held[pl.ds(0, BAND), lanes] = field(top_ref[0, j], coef_top_ref[0], BAND, 0, j)
            held[pl.ds(BAND, lat_here), lanes] = field(inside_ref[j], coef_ref, lat_here, BAND, j)
            held[pl.ds(below, BAND), lanes] = field(
                bottom_ref[0, j], coef_bottom_ref[0], BAND, below, j
            )
        merid = jnp.dot(band_ref[...], held[...], preferred_element_type=F32).astype(BF16)
        for side in range(2):
            out_ref[2 * pair + side] = jnp.dot(
                merid[:, side * LANES : (side + 1) * LANES],
                level_ref[...],
                preferred_element_type=F32,
            ).astype(BF16)


def run_combine(inside, inside_halo, coef, coef_halo, entry, band_tile, level_map, levels):
    lon_here, lat_here, _ = inside.shape
    batch = 8
    per_tile = LANES // levels

    def tile_of(t):
        return t * batch // per_tile

    return pl.pallas_call(
        functools.partial(combine_kernel, batch, levels),
        name="band_product",
        grid=(lon_here // batch,),
        out_shape=jax.ShapeDtypeStruct((lon_here, lat_here, LANES), BF16),
        in_specs=[
            pl.BlockSpec((batch, lat_here, LANES), lambda t: (t, 0, 0)),
            pl.BlockSpec((1, batch, BAND, LANES), lambda t: (0, t, 0, 0)),
            pl.BlockSpec((1, batch, BAND, LANES), lambda t: (1, t, 0, 0)),
            pl.BlockSpec((2, lat_here, LANES), lambda t: (0, 0, tile_of(t))),
            pl.BlockSpec((1, 2, BAND, LANES), lambda t: (0, 0, 0, tile_of(t))),
            pl.BlockSpec((1, 2, BAND, LANES), lambda t: (1, 0, 0, tile_of(t))),
            pl.BlockSpec((2, lat_here + 2 * BAND, LANES), lambda t: (0, 0, 0)),
            pl.BlockSpec(band_tile.shape, lambda t: (0, 0)),
            pl.BlockSpec(level_map.shape, lambda t: (0, 0)),
        ],
        out_specs=pl.BlockSpec((batch, lat_here, LANES), lambda t: (t, 0, 0)),
        scratch_shapes=[pltpu.VMEM((2, lat_here + 2 * BAND, 2 * LANES), BF16)],
        compiler_params=pltpu.CompilerParams(vmem_limit_bytes=24 << 20),
    )(inside, inside_halo, inside_halo, coef, coef_halo, coef_halo, entry, band_tile, level_map)


def solution(mesh):
    def per_device(sketch_bits, rates, merid_matrix, vert_matrix):
        levels = vert_matrix.shape[0]
        ends, inside, coef, coef_small = run_filters(rates, sketch_bits)
        entry, inside_halo, coef_halo, band_tile, level_map = run_exchange(
            mesh, levels, ends, inside, coef_small, merid_matrix, vert_matrix
        )
        return run_combine(
            inside, inside_halo, coef, coef_halo, entry, band_tile, level_map, levels
        )

    in_specs = (P("lon", "lat", None), P("lon", None, "lat"), P("lat", None), P())
    out_specs = P("lon", "lat", None)
    return jax.shard_map(
        per_device, mesh=mesh, in_specs=in_specs, out_specs=out_specs, check_vma=False
    )
```

```python
import functools

import jax
import jax.numpy as jnp
from jax import lax
from jax.experimental import pallas as pl
from jax.experimental.pallas import tpu as pltpu
from jax.sharding import PartitionSpec as P

BAND = 96
LANES = 128
F32 = jnp.float32
BF16 = jnp.bfloat16
MESH = pl.DeviceIdType.MESH


def loss_of(rate):
    factors = [1.0]
    for order in range(2, 13):
        factors.append(-factors[-1] / order)
    total = jnp.full_like(rate, factors[-1])
    for factor in reversed(factors[:-1]):
        total = total * rate + factor
    return rate * total


def filter_kernel(
    rates_hbm,
    bits_hbm,
    ends_ref,
    inside_ref,
    inside_small_ref,
    coef_ref,
    coef_small_ref,
    rates_ref,
    bits,
    even,
    odd,
    state_ref,
    lev,
    sems,
):
    lon_here, levels, lat_here = rates_ref.shape
    each = LANES // levels
    width = 2 * LANES
    second = lat_here - LANES
    rates_copy = pltpu.make_async_copy(rates_hbm, rates_ref, sems.at[0])
    bits_copy = pltpu.make_async_copy(bits_hbm, bits, sems.at[1])
    rates_copy.start()
    bits_copy.start()
    rates_copy.wait()

    rate = jnp.concatenate([rates_ref[:, :, :LANES], rates_ref[:, :, second:]], axis=2)
    loss = loss_of(rate)
    squared = loss * (2.0 - loss)
    decay = 1.0 - loss
    lev[0] = decay
    lev[1] = jnp.sqrt(squared)
    lev[2] = squared * lax.rsqrt(1.0 + decay * decay)
    lev[3] = loss

    passed = jnp.ones((levels, width), F32)
    lost = jnp.zeros((levels, width), F32)
    for i in range(lon_here):
        passed = lev[0, i] * passed
        lost = lost + lev[3, i] * (1.0 - lost)
        coef_ref[0, i] = passed
    coef = jnp.zeros((levels, width), F32)
    kept = jnp.ones((levels, width), F32)
    for i in reversed(range(lon_here)):
        here = lev[0, i]
        coef = here * coef + lev[2, i] * coef_ref[0, i]
        kept = here * kept
        coef_ref[0, i] = coef
        coef_ref[1, i] = kept
    for which in range(2):
        coef_small_ref[which] = coef_ref[which].reshape(lon_here * levels, width).astype(BF16)

    def part(level):
        return pl.ds(level * each, each)

    def wide(which, i, level):
        return jnp.broadcast_to(lev[which, i, pl.ds(level, 1), :], (each, width))

    def turn(i, ref):
        ref[:, :LANES] = bits[i, :LANES, :].T
        ref[:, LANES:] = bits[i, second:, :].T

    def forward(i, turned):
        for level in range(levels):
            gain = wide(1, i, level)
            state = wide(0, i, level) * state_ref[part(level), :]
            state = state + jnp.where(turned[part(level), :] > 0, gain, -gain)
            inside_ref[i, part(level), :] = state
            state_ref[part(level), :] = state

    def backward(i):
        for level in range(levels):
            state = wide(0, i, level) * state_ref[part(level), :]
            state = state + wide(2, i, level) * inside_ref[i, part(level), :]
            inside_ref[i, part(level), :] = state
            inside_small_ref[i, part(level), :] = state.astype(BF16)
            state_ref[part(level), :] = state

    def put_ends(first):
        for level in range(levels):
            ends_ref[level, pl.ds(first, each), :] = state_ref[part(level), :]

    bits_copy.wait()
    state_ref[...] = jnp.zeros(state_ref.shape, F32)
    turn(0, even)

    def go_east(k, _):
        turn(2 * k + 1, odd)
        forward(2 * k, even)
        turn(jnp.minimum(2 * k + 2, lon_here - 1), even)
        forward(2 * k + 1, odd)
        return 0

    lax.fori_loop(0, lon_here // 2, go_east, 0)
    put_ends(0)
    state_ref[...] = jnp.zeros(state_ref.shape, F32)

    def go_west(k, _):
        backward(lon_here - 1 - 2 * k)
        backward(lon_here - 2 - 2 * k)
        return 0

    lax.fori_loop(0, lon_here // 2, go_west, 0)
    put_ends(each)
    for level in range(levels):
        ends_ref[level, pl.ds(2 * each, 8), :] = jnp.concatenate(
            [lost[level : level + 1], coef[level : level + 1], jnp.zeros((6, width), F32)], axis=0
        )


def run_filters(rates, bits):
    lon_here, levels, lat_here = rates.shape
    vmem = pl.BlockSpec(memory_space=pltpu.VMEM)
    hbm = pl.BlockSpec(memory_space=pltpu.HBM)
    width = 2 * LANES
    return pl.pallas_call(
        filter_kernel,
        name="zonal_filters",
        out_shape=(
            jax.ShapeDtypeStruct((levels, 2 * LANES // levels + 8, width), F32),
            jax.ShapeDtypeStruct((lon_here, LANES, width), F32),
            jax.ShapeDtypeStruct((lon_here, LANES, width), BF16),
            jax.ShapeDtypeStruct((2, lon_here, levels, width), F32),
            jax.ShapeDtypeStruct((2, lon_here * levels, width), BF16),
        ),
        in_specs=[hbm, hbm],
        out_specs=(vmem,) * 5,
        scratch_shapes=[
            pltpu.VMEM((lon_here, levels, lat_here), F32),
            pltpu.VMEM((lon_here, lat_here, LANES), jnp.int32),
            pltpu.VMEM((LANES, width), jnp.int32),
            pltpu.VMEM((LANES, width), jnp.int32),
            pltpu.VMEM((LANES, width), F32),
            pltpu.VMEM((4, lon_here, levels, width), F32),
            pltpu.SemaphoreType.DMA((2,)),
        ],
        compiler_params=pltpu.CompilerParams(vmem_limit_bytes=32 << 20),
    )(
        pltpu.with_memory_space_constraint(rates, pltpu.HBM),
        pltpu.with_memory_space_constraint(bits, pltpu.HBM),
    )


def compose(near, far):
    loss_a, cross_a, east_a, west_a = near
    loss_b, cross_b, east_b, west_b = far
    keep_a, keep_b = 1.0 - loss_a, 1.0 - loss_b
    return (
        loss_a + keep_a * loss_b,
        cross_a + keep_a * cross_b * keep_a,
        east_b + keep_b * east_a,
        west_a + keep_a * (west_b + cross_b * east_a),
    )


def exchange_kernel(
    inner,
    outer,
    lats,
    ends_ref,
    inside_hbm,
    coef_hbm,
    merid_ref,
    vert_ref,
    entry_ref,
    inside_halo,
    coef_halo,
    band_ref,
    level_ref,
    coef_landing,
    parts,
    joined,
    groups,
    solved,
    send_sem,
    recv_sem,
    halo_send,
    halo_recv,
):
    lon = lax.axis_index("lon")
    lat = lax.axis_index("lat")
    place, group = lon % inner, lon // inner
    lat_here = band_ref.shape[0]
    each = LANES // inner
    has_prev, has_next = lat > 0, lat < lats - 1
    prev_lat, next_lat = jnp.maximum(lat - 1, 0), jnp.minimum(lat + 1, lats - 1)

    def device(lon_id, lat_id):
        return {"lon": lon_id, "lat": lat_id}

    def mate(k):
        return (place + k) % inner

    def mate_lon(k):
        return group * inner + mate(k)

    def remote_lon(k):
        return (group + k) % outer * inner + place

    barrier = pltpu.get_barrier_semaphore()

    def greet(lon_id, lat_id):
        pl.semaphore_signal(barrier, inc=1, device_id=device(lon_id, lat_id), device_id_type=MESH)

    def greet_mates(k, _):
        greet(mate_lon(k), lat)
        return 0

    def greet_groups(k, _):
        greet(remote_lon(k), lat)
        return 0

    lax.fori_loop(1, inner, greet_mates, 0)
    lax.fori_loop(1, outer, greet_groups, 0)

    @pl.when(has_prev)
    def _():
        def greet_side(k, _):
            greet(group * inner + k, prev_lat)
            return 0

        lax.fori_loop(0, inner, greet_side, 0)

    @pl.when(has_next)
    def _():
        def greet_side(k, _):
            greet(group * inner + k, next_lat)
            return 0

        lax.fori_loop(0, inner, greet_side, 0)

    lat_all = merid_ref.shape[1]
    spans = (lat_all, 4 * LANES)
    source = lax.broadcasted_iota(jnp.int32, spans, 0)
    target = lax.broadcasted_iota(jnp.int32, spans, 1)
    second = lat_here - LANES
    own = lat * lat_here + jnp.where(target < LANES, target, target - LANES + second)
    before = (lat - 1) * lat_here + target - 2 * LANES + second
    after = (lat + 1) * lat_here + target - 3 * LANES
    wanted = jnp.where(target < 2 * LANES, own, jnp.where(target < 3 * LANES, before, after))
    repeated = jnp.logical_and(target >= LANES, target < 2 * LANES - second)
    hit = jnp.logical_and(source == wanted, jnp.logical_not(repeated))
    pick = jnp.where(hit, 1.0, 0.0).astype(BF16)
    band_ref[...] = jnp.dot(merid_ref[...], pick, preferred_element_type=F32).astype(BF16)
    levels = vert_ref.shape[0]
    columns_each = LANES // levels
    column = lax.broadcasted_iota(jnp.int32, (LANES, levels), 0)
    level = lax.broadcasted_iota(jnp.int32, (LANES, levels), 1)
    member = jnp.where(column // columns_each == level, 1.0, 0.0).astype(BF16)
    along = (((1,), (1,)), ((), ()))
    by_row = lax.dot_general(member, vert_ref[...], along, preferred_element_type=F32)
    full = lax.dot_general(by_row.astype(BF16), member, along, preferred_element_type=F32)
    row = lax.broadcasted_iota(jnp.int32, (LANES, LANES), 0)
    col = lax.broadcasted_iota(jnp.int32, (LANES, LANES), 1)
    same = row % columns_each == col % columns_each
    level_ref[...] = jnp.where(same, full, 0.0).astype(BF16)

    def clear(slot):
        def clear_lon(i, _):
            inside_halo[slot, i] = jnp.zeros(inside_halo.shape[2:], BF16)
            return 0

        lax.fori_loop(0, inside_halo.shape[1], clear_lon, 0)
        coef_halo[slot] = jnp.zeros(coef_halo.shape[1:], F32)
        lanes = pl.ds((2 + slot) * LANES, LANES)
        entry_ref[:, :, lanes] = jnp.zeros((2, LANES, LANES), F32)

    @pl.when(jnp.logical_not(has_prev))
    def _():
        clear(0)

    @pl.when(jnp.logical_not(has_next))
    def _():
        clear(1)

    sides = has_prev.astype(jnp.int32) + has_next.astype(jnp.int32)
    pl.semaphore_wait(barrier, inner - 1 + outer - 1 + inner * sides)

    def part_copy(k):
        return pltpu.make_async_remote_copy(
            src_ref=ends_ref.at[mate(k)],
            dst_ref=parts.at[place],
            send_sem=send_sem.at[0, k],
            recv_sem=recv_sem.at[0, place],
            device_id=device(mate_lon(k), lat),
            device_id_type=MESH,
        )

    def part_arrival(k):
        return pltpu.make_async_remote_copy(
            src_ref=ends_ref.at[mate(k)],
            dst_ref=parts.at[mate(k)],
            send_sem=send_sem.at[0, k],
            recv_sem=recv_sem.at[0, mate(k)],
            device_id=device(mate_lon(k), lat),
            device_id_type=MESH,
        )

    def send_part(k, _):
        part_copy(k).start()
        return 0

    lax.fori_loop(1, inner, send_part, 0)
    parts[place] = ends_ref[place]

    def side_copies(first, slot, lat_id, base):
        return [
            pltpu.make_async_remote_copy(
                src_ref=inside_hbm.at[:, :, pl.ds(first, LANES)],
                dst_ref=inside_halo.at[slot],
                send_sem=halo_send.at[base],
                recv_sem=halo_recv.at[slot * 2],
                device_id=device(lon, lat_id),
                device_id_type=MESH,
            ),
            pltpu.make_async_remote_copy(
                src_ref=coef_hbm.at[:, :, pl.ds(first, LANES)],
                dst_ref=coef_landing.at[slot],
                send_sem=halo_send.at[base + 1],
                recv_sem=halo_recv.at[slot * 2 + 1],
                device_id=device(lon, lat_id),
                device_id_type=MESH,
            ),
        ]

    @pl.when(has_prev)
    def _():
        for copy in side_copies(0, 1, prev_lat, 0):
            copy.start()

    @pl.when(has_next)
    def _():
        for copy in side_copies(LANES, 0, next_lat, 2):
            copy.start()

    def wait_part(k, _):
        part_arrival(k).wait_recv()
        return 0

    lax.fori_loop(1, inner, wait_part, 0)

    def map_of(ref, index):
        value = ref[index]
        own = 2 * each
        return value[own : own + 1], value[own + 1 : own + 2], value[:each], value[each:own]

    def join(p, near):
        return compose(near, map_of(parts, p))

    loss, cross, east, west = lax.fori_loop(1, inner, join, map_of(parts, 0))
    zero_rows = jnp.zeros((6, 2 * LANES), F32)
    whole = jnp.concatenate([east, west, loss, cross, zero_rows], axis=0)
    joined[...] = whole

    def group_copy(k):
        return pltpu.make_async_remote_copy(
            src_ref=joined,
            dst_ref=groups.at[group],
            send_sem=send_sem.at[1, k],
            recv_sem=recv_sem.at[1, group],
            device_id=device(remote_lon(k), lat),
            device_id_type=MESH,
        )

    def group_arrival(k):
        other = (group + k) % outer
        return pltpu.make_async_remote_copy(
            src_ref=joined,
            dst_ref=groups.at[other],
            send_sem=send_sem.at[1, k],
            recv_sem=recv_sem.at[1, other],
            device_id=device(remote_lon(k), lat),
            device_id_type=MESH,
        )

    def send_group(k, _):
        group_copy(k).start()
        return 0

    lax.fori_loop(1, outer, send_group, 0)
    groups[group] = whole

    def wait_group(k, _):
        group_arrival(k).wait_recv()
        return 0

    lax.fori_loop(1, outer, wait_group, 0)

    zeros = jnp.zeros((each, 2 * LANES), F32)
    none = jnp.zeros((1, 2 * LANES), F32)

    def whole_east(z, carry):
        state, lost = carry
        loss_z, _, east_z, _ = map_of(groups, z)
        return east_z + state - loss_z * state, lost + loss_z - lost * loss_z

    end_state, lost = lax.fori_loop(0, outer, whole_east, (zeros, none))
    first_east = end_state / lost

    def whole_west(z, carry):
        state, kept, east_now = carry
        loss_z, cross_z, east_z, west_z = map_of(groups, z)
        keep_z = 1.0 - loss_z
        state = state + kept * (west_z + cross_z * east_now)
        return state, kept * keep_z, east_z + keep_z * east_now

    west_total, _, _ = lax.fori_loop(0, outer, whole_west, (zeros, none + 1.0, first_east))
    last_west = west_total / lost

    def to_group(z, state):
        loss_z, _, east_z, _ = map_of(groups, z)
        return east_z + state - loss_z * state

    east_here = lax.fori_loop(0, group, to_group, first_east)

    def west_before(z, carry):
        state, kept, east_now = carry
        loss_z, cross_z, east_z, west_z = map_of(groups, z)
        keep_z = 1.0 - loss_z
        state = state + kept * (west_z + cross_z * east_now)
        return state, kept * keep_z, east_z + keep_z * east_now

    _, _, east_after = lax.fori_loop(group, group + 1, west_before, (zeros, none + 1.0, east_here))
    state, kept, _ = lax.fori_loop(group + 1, outer, west_before, (zeros, none + 1.0, east_after))
    west_here = state + kept * last_west

    def inner_east(p, state):
        loss_p, _, east_p, _ = map_of(parts, p)
        solved[p, 0] = state
        return east_p + state - loss_p * state

    lax.fori_loop(0, inner, inner_east, east_here)

    def inner_west(k, state):
        p = inner - 1 - k
        loss_p, cross_p, _, west_p = map_of(parts, p)
        solved[p, 1] = state
        return west_p + cross_p * solved[p, 0] + state - loss_p * state

    lax.fori_loop(0, inner, inner_west, west_here)

    def part_of(index):
        return pl.ds(pl.multiple_of(index * each, each), each)

    def entry_copy(k):
        return pltpu.make_async_remote_copy(
            src_ref=solved.at[mate(k)],
            dst_ref=entry_ref.at[:, part_of(place), pl.ds(0, 2 * LANES)],
            send_sem=send_sem.at[2, k],
            recv_sem=recv_sem.at[2, place],
            device_id=device(mate_lon(k), lat),
            device_id_type=MESH,
        )

    def entry_arrival(k):
        return pltpu.make_async_remote_copy(
            src_ref=solved.at[mate(k)],
            dst_ref=entry_ref.at[:, part_of(mate(k)), pl.ds(0, 2 * LANES)],
            send_sem=send_sem.at[2, k],
            recv_sem=recv_sem.at[2, mate(k)],
            device_id=device(mate_lon(k), lat),
            device_id_type=MESH,
        )

    def side_copy(p, slot, lat_id):
        return pltpu.make_async_remote_copy(
            src_ref=solved.at[p, :, :, pl.ds((1 - slot) * LANES, LANES)],
            dst_ref=entry_ref.at[:, part_of(place), pl.ds((2 + slot) * LANES, LANES)],
            send_sem=send_sem.at[3 + slot, p],
            recv_sem=recv_sem.at[3 + slot, place],
            device_id=device(group * inner + p, lat_id),
            device_id_type=MESH,
        )

    def side_arrival(p, slot):
        return pltpu.make_async_remote_copy(
            src_ref=solved.at[p, :, :, pl.ds((1 - slot) * LANES, LANES)],
            dst_ref=entry_ref.at[:, part_of(p), pl.ds((2 + slot) * LANES, LANES)],
            send_sem=send_sem.at[3 + slot, p],
            recv_sem=recv_sem.at[3 + slot, p],
            device_id=device(group * inner + p, lat),
            device_id_type=MESH,
        )

    @pl.when(has_prev)
    def _():
        def send_side(p, _):
            side_copy(p, 1, prev_lat).start()
            return 0

        lax.fori_loop(0, inner, send_side, 0)

    @pl.when(has_next)
    def _():
        def send_side(p, _):
            side_copy(p, 0, next_lat).start()
            return 0

        lax.fori_loop(0, inner, send_side, 0)

    def send_entry(k, _):
        entry_copy(k).start()
        return 0

    lax.fori_loop(1, inner, send_entry, 0)
    entry_ref[:, part_of(place), pl.ds(0, 2 * LANES)] = solved[place]

    def wait_entry(k, _):
        entry_arrival(k).wait_recv()
        return 0

    lax.fori_loop(1, inner, wait_entry, 0)

    @pl.when(has_prev)
    def _():
        def wait_side(p, _):
            side_arrival(p, 0).wait_recv()
            return 0

        lax.fori_loop(0, inner, wait_side, 0)

    @pl.when(has_next)
    def _():
        def wait_side(p, _):
            side_arrival(p, 1).wait_recv()
            return 0

        lax.fori_loop(0, inner, wait_side, 0)

    @pl.when(has_prev)
    def _():
        inside_copy, coef_copy = side_copies(0, 0, prev_lat, 0)
        coef_copy.wait_recv()
        coef_halo[0] = coef_landing[0].astype(F32)
        inside_copy.wait_recv()
        for copy in side_copies(0, 1, prev_lat, 0):
            copy.wait_send()

    @pl.when(has_next)
    def _():
        inside_copy, coef_copy = side_copies(LANES, 1, next_lat, 2)
        coef_copy.wait_recv()
        coef_halo[1] = coef_landing[1].astype(F32)
        inside_copy.wait_recv()
        for copy in side_copies(LANES, 0, next_lat, 2):
            copy.wait_send()

    def drain_inner(k, _):
        part_copy(k).wait_send()
        entry_copy(k).wait_send()
        return 0

    def drain_outer(k, _):
        group_copy(k).wait_send()
        return 0

    lax.fori_loop(1, inner, drain_inner, 0)
    lax.fori_loop(1, outer, drain_outer, 0)

    @pl.when(has_prev)
    def _():
        def drain(p, _):
            side_copy(p, 1, prev_lat).wait_send()
            return 0

        lax.fori_loop(0, inner, drain, 0)

    @pl.when(has_next)
    def _():
        def drain(p, _):
            side_copy(p, 0, next_lat).wait_send()
            return 0

        lax.fori_loop(0, inner, drain, 0)


def run_exchange(mesh, ends, inside, coef_small, merid, vert):
    lons, lats = mesh.shape["lon"], mesh.shape["lat"]
    inner, height, width = ends.shape
    outer = lons // inner
    lat_here = merid.shape[0]
    lon_here = inside.shape[0]
    vmem = pl.BlockSpec(memory_space=pltpu.VMEM)
    hbm = pl.BlockSpec(memory_space=pl.ANY)
    most = max(inner, outer)
    return pl.pallas_call(
        functools.partial(exchange_kernel, inner, outer, lats),
        name="loop_exchange",
        out_shape=(
            jax.ShapeDtypeStruct((2, LANES, 4 * LANES), F32),
            jax.ShapeDtypeStruct((2, lon_here, LANES, LANES), BF16),
            jax.ShapeDtypeStruct((2, 2, coef_small.shape[1], LANES), F32),
            jax.ShapeDtypeStruct((lat_here, 4 * LANES), BF16),
            jax.ShapeDtypeStruct((LANES, LANES), BF16),
        ),
        in_specs=[vmem, hbm, hbm, vmem, vmem],
        out_specs=(vmem, vmem, vmem, vmem, vmem),
        scratch_shapes=[
            pltpu.VMEM((2, 2, coef_small.shape[1], LANES), BF16),
            pltpu.VMEM((inner, height, width), F32),
            pltpu.VMEM((height, width), F32),
            pltpu.VMEM((outer, height, width), F32),
            pltpu.VMEM((inner, 2, LANES // inner, width), F32),
            pltpu.SemaphoreType.DMA((5, most)),
            pltpu.SemaphoreType.DMA((5, most)),
            pltpu.SemaphoreType.DMA((4,)),
            pltpu.SemaphoreType.DMA((4,)),
        ],
        compiler_params=pltpu.CompilerParams(
            collective_id=0, has_side_effects=True, vmem_limit_bytes=24 << 20
        ),
    )(ends, inside, coef_small, merid, vert)


def combine_kernel(
    batch,
    levels,
    inside_ref,
    before_ref,
    after_ref,
    coef_ref,
    coef_before_ref,
    coef_after_ref,
    entry_ref,
    band_ref,
    level_ref,
    out_ref,
    zonal,
):
    each = LANES // levels
    group = 4
    along = (((1,), (1,)), ((), ()))

    def fill(first):
        for level in range(levels):
            rows = pl.ds(level * each, each)
            for tile in range(4):
                lanes = pl.ds(tile * LANES, LANES)
                east, west = entry_ref[0, rows, lanes], entry_ref[1, rows, lanes]
                for j in range(first, first + group):
                    row = j * levels + level
                    if tile < 2:
                        inside = inside_ref[j, rows, lanes]
                        cross = coef_ref[0, j, pl.ds(level, 1), lanes]
                        kept = coef_ref[1, j, pl.ds(level, 1), lanes]
                    else:
                        halo, coef = (
                            (before_ref, coef_before_ref),
                            (after_ref, coef_after_ref),
                        )[tile - 2]
                        inside = halo[0, j, rows, :].astype(F32)
                        cross = coef[0, 0, pl.ds(row, 1), :]
                        kept = coef[0, 1, pl.ds(row, 1), :]
                    field = inside + cross * east + kept * west
                    zonal[j // 2, pl.ds(j % 2 * LANES + level * each, each), lanes] = (
                        field.astype(BF16)
                    )

    def multiply(first):
        for pair in range(first // 2, (first + group) // 2):
            merid = lax.dot_general(
                band_ref[...], zonal[pair], along, preferred_element_type=F32
            ).astype(BF16)
            for side in range(2):
                out_ref[2 * pair + side] = jnp.dot(
                    merid[:, side * LANES : (side + 1) * LANES],
                    level_ref[...],
                    preferred_element_type=F32,
                ).astype(BF16)

    fill(0)
    for first in range(group, batch, group):
        fill(first)
        multiply(first - group)
    multiply(batch - group)


def run_combine(inside, inside_halo, coef, coef_halo, entry, band_tile, level_map):
    lon_here, _, width = inside.shape
    levels = coef.shape[2]
    lat_here = band_tile.shape[0]
    batch = 8
    return pl.pallas_call(
        functools.partial(combine_kernel, batch, levels),
        name="band_product",
        grid=(lon_here // batch,),
        out_shape=jax.ShapeDtypeStruct((lon_here, lat_here, LANES), BF16),
        in_specs=[
            pl.BlockSpec((batch, LANES, width), lambda t: (t, 0, 0)),
            pl.BlockSpec((1, batch, LANES, LANES), lambda t: (0, t, 0, 0)),
            pl.BlockSpec((1, batch, LANES, LANES), lambda t: (1, t, 0, 0)),
            pl.BlockSpec((2, batch, levels, width), lambda t: (0, t, 0, 0)),
            pl.BlockSpec((1, 2, batch * levels, LANES), lambda t: (0, 0, t, 0)),
            pl.BlockSpec((1, 2, batch * levels, LANES), lambda t: (1, 0, t, 0)),
            pl.BlockSpec(entry.shape, lambda t: (0, 0, 0)),
            pl.BlockSpec(band_tile.shape, lambda t: (0, 0)),
            pl.BlockSpec(level_map.shape, lambda t: (0, 0)),
        ],
        out_specs=pl.BlockSpec((batch, lat_here, LANES), lambda t: (t, 0, 0)),
        scratch_shapes=[pltpu.VMEM((batch // 2, 2 * LANES, 4 * LANES), BF16)],
        compiler_params=pltpu.CompilerParams(vmem_limit_bytes=20 << 20),
    )(inside, inside_halo, inside_halo, coef, coef_halo, coef_halo, entry, band_tile, level_map)


def solution(mesh):
    def per_device(sketch_bits, rates, merid_matrix, vert_matrix):
        ends, inside, inside_small, coef, coef_small = run_filters(rates, sketch_bits)
        entry, inside_halo, coef_halo, band_tile, level_map = run_exchange(
            mesh, ends, inside_small, coef_small, merid_matrix, vert_matrix
        )
        return run_combine(inside, inside_halo, coef, coef_halo, entry, band_tile, level_map)

    in_specs = (P("lon", "lat", None), P("lon", None, "lat"), P("lat", None), P())
    out_specs = P("lon", "lat", None)
    return jax.shard_map(
        per_device, mesh=mesh, in_specs=in_specs, out_specs=out_specs, check_vma=False
    )
```
